32 devices in a mesh: rcv: 8 (over z, y), src: 4 (over x, core).
Axes of the slice: x: 2, y: 2, z: 4, core: 2. Of those that a mesh axis runs over, the one named last changes fastest.
Arguments:
- k_op: bfloat16 [2, 3072, 3072], P(None, 'rcv', 'src'), may hold values from -0.078125 to 0.078125
- data: bfloat16 [2, 3072, 3072], P(None, 'rcv', 'src'), may hold values from -6 to 6
- factor: bfloat16 [2, 4, 768, 128], P(None, 'src', 'rcv'), may hold values from -1.796875 to 1.796875
Outputs:
- gradient: float32 [2, 4, 768, 128], P(None, 'src', 'rcv')
The draws below stay inside these ranges and needn't reach their ends.
All inputs are finite; a program needn't handle non-finite values.
Results may differ from the reference program's by a relative error of at most 0.0019.
Values may be sent and summed in bfloat16 or wider, within the bound.
A program may use at most 64 MiB of HBM per device.

```python
import math
import jax
import jax.numpy as jnp
from jax import lax

ROWS_DEV = 384
COLS_DEV = 768
RANK = 128
NREC = 3072
NSRC = 3072
BLOCKS = 4


def with_spikes(values, own_key, source, target, shards_of, factor):
    owner, partner = [(jnp.arange(values.shape[dim]) // (values.shape[dim] // shards_of)).reshape([-1 if axis == dim else 1 for axis in range(values.ndim)]) for dim in (source, target)]
    chosen = jax.random.permutation(own_key, shards_of)[partner]
    strong = (owner == chosen) | (owner == (partner + shards_of // 2) % shards_of)
    return jnp.where(strong, factor * values, values)


def block_scale(rng, shape, pieces, smallest, largest):
    def one(position, parts):
        draws = jax.random.uniform(jax.random.fold_in(jax.random.fold_in(rng, 6), position), (parts,), jnp.float32, smallest / len(pieces), largest / len(pieces))
        return jnp.repeat(jnp.exp(draws), shape[position] // parts).reshape((-1,) + (1,) * (len(shape) - position - 1))

    level = one(*pieces[0])
    for cut in pieces[1:]:
        level = level * one(*cut)
    return level


def scatter_about(own_key, extent, width, reach, shards=(), dtype=jnp.bfloat16):
    drawn = jax.random.normal(own_key, extent, jnp.float32) * width
    if len(shards) > 0:
        drawn = block_scale(own_key, extent, shards, -0.22, 0.18) * drawn
    return jnp.clip(drawn, min=-reach, max=reach).astype(dtype)


def heavy_noise(stream_key, extent, width, most, cuts, heavy, kind=jnp.bfloat16):
    array = width * jax.random.normal(stream_key, extent, jnp.float32)
    if cuts:
        array = array * block_scale(stream_key, extent, cuts, -0.22, 0.18)
    return jnp.clip(with_spikes(array, jax.random.fold_in(stream_key, 3), *heavy), -most, most).astype(kind)


def setup_inputs(seed: int = 0) -> dict:
    key_of = jax.random.split(jax.random.key(seed), 4)
    return {
        "k_op": scatter_about(key_of[0], (2, NREC, NSRC), (2 * NSRC) ** -0.5, 0.078125, ((1, 8), (2, 4))),
        "data": heavy_noise(key_of[1], (2, NREC, NSRC), 1.0, 6.0, ((1, 8), (2, 4)), (1, 2, 8, 2.0)),
        "factor": scatter_about(key_of[2], (2, BLOCKS, COLS_DEV, RANK), 0.3, 1.796875, ((1, 4), (2, 8))),
    }


def plain_dot(left, right):
    return jnp.dot(left, right, preferred_element_type=jnp.float32)

def reference(k_op, data, factor):
    whole_factor = factor.reshape(2, NSRC, RANK)
    factor_real = whole_factor[0]
    factor_imaginary = whole_factor[1]
    kernel_real = k_op[0]
    kernel_imaginary = k_op[1]
    modeled_real = (plain_dot(kernel_real, factor_real) - plain_dot(kernel_imaginary, factor_imaginary)).astype(jnp.bfloat16)
    modeled_imaginary = (plain_dot(kernel_real, factor_imaginary) + plain_dot(kernel_imaginary, factor_real)).astype(jnp.bfloat16)
    count = NREC // ROWS_DEV
    blocks = (kernel_real.reshape(count, ROWS_DEV, NSRC), kernel_imaginary.reshape(count, ROWS_DEV, NSRC), data[0].reshape(count, ROWS_DEV, NSRC), data[1].reshape(count, ROWS_DEV, NSRC), modeled_real.reshape(count, ROWS_DEV, RANK), modeled_imaginary.reshape(count, ROWS_DEV, RANK))

    def advance(running, block):
        rows_real, rows_imaginary, observed_real, observed_imaginary, model_real, model_imaginary = block
        error_real = (plain_dot(model_real, factor_real.T) - plain_dot(model_imaginary, factor_imaginary.T) - observed_real.astype(jnp.float32)).astype(jnp.bfloat16)
        error_imaginary = (plain_dot(model_real, factor_imaginary.T) + plain_dot(model_imaginary, factor_real.T) - observed_imaginary.astype(jnp.float32)).astype(jnp.bfloat16)
        weighted_real = (plain_dot(error_real, factor_real) + plain_dot(error_imaginary, factor_imaginary)).astype(jnp.bfloat16)
        weighted_imaginary = (plain_dot(error_imaginary, factor_real) - plain_dot(error_real, factor_imaginary)).astype(jnp.bfloat16)
        grad_real = plain_dot(rows_real.T, weighted_real) + plain_dot(rows_imaginary.T, weighted_imaginary) + plain_dot(error_real.T, model_real) + plain_dot(error_imaginary.T, model_imaginary)
        grad_imaginary = plain_dot(rows_real.T, weighted_imaginary) - plain_dot(rows_imaginary.T, weighted_real) + plain_dot(error_imaginary.T, model_real) - plain_dot(error_real.T, model_imaginary)
        return ((running[0] + grad_real, running[1] + grad_imaginary), None)
    start = (jnp.zeros((NSRC, RANK), jnp.float32), jnp.zeros((NSRC, RANK), jnp.float32))
    summed, unused = lax.scan(advance, start, blocks)
    scaling = 1.0 / math.sqrt(NREC)
    gradient = jnp.stack([summed[0], summed[1]]) * scaling
    return gradient.reshape(2, NSRC // COLS_DEV, COLS_DEV, RANK)
```

```python
import functools
import math

import jax
import jax.numpy as jnp
from jax import lax
from jax.experimental import pallas as pl
from jax.experimental.pallas import tpu as pltpu
from jax.sharding import PartitionSpec as P

F32 = jnp.float32
BF16 = jnp.bfloat16


def dot(left, right):
    return jnp.dot(left, right, preferred_element_type=F32)


def gram(cat):
    rank = cat.shape[1] // 2
    full = lax.dot_general(cat, cat, (((0,), (0,)), ((), ())), preferred_element_type=F32)
    real = full[:rank, :rank] + full[rank:, rank:]
    imaginary = full[rank:, :rank] - full[:rank, rank:]
    return jnp.concatenate([real, imaginary], axis=1)


def complex_right(cat):
    rank = cat.shape[1] // 2
    real, imaginary = cat[:, :rank], cat[:, rank:]
    full = jnp.concatenate([cat, jnp.concatenate([-imaginary, real], axis=1)], axis=0)
    high = full.astype(BF16)
    low = (full - high.astype(F32)).astype(BF16)
    return high, low


def regroup(values, shape):
    if shape[-2] % 16 == 0 and values.shape[-2] % 16 == 0:
        return values.reshape(shape)
    return values.astype(F32).reshape(shape).astype(BF16)


def kernel(
    nz, nx, scaling,
    k_hbm, d_hbm, q_hbm, o_ref,
    a_buf, k_vm, d_vm, xt,
    g_loc, g_rx, g_xtx, g_xrx, g_fin,
    c_tx, c_rx, z_xtx, z_xrx, v_xtx, v_xrx, zw,
    y_tx, y_rx, t_tx, t_rx,
    lsem, ssem, rsem,
):
    rcv, src = lax.axis_index("rcv"), lax.axis_index("src")
    z, y = rcv // 2, rcv % 2
    x, c = src // 2, src % 2
    ypeer = {"rcv": z * 2 + 1 - y}
    cpeer = {"src": x * 2 + 1 - c}
    zpeers = [{"rcv": lax.rem(z + d, nz) * 2 + y} for d in range(1, nz)]
    xpeers = [{"src": lax.rem(x + d, nx) * 2 + c} for d in range(1, nx)]
    everyone = [ypeer, cpeer] + zpeers + xpeers
    rows, cols = k_vm.shape[1], k_vm.shape[2]
    half = rows // 2
    rank = q_hbm.shape[3]
    own = q_hbm.shape[2]
    ghalf = rank // 2

    counter = [0]
    started = []

    def remote(source, target, peer):
        at = counter[0]
        counter[0] += 1
        copy = pltpu.make_async_remote_copy(
            src_ref=source, dst_ref=target, send_sem=ssem.at[at], recv_sem=rsem.at[at],
            device_id=peer, device_id_type=pl.DeviceIdType.MESH,
        )
        copy.start()
        started.append(copy)
        return copy

    loads = [
        pltpu.make_async_copy(q_hbm.at[0, 0], a_buf.at[z, y, :, pl.ds(0, rank)], lsem.at[0]),
        pltpu.make_async_copy(q_hbm.at[1, 0], a_buf.at[z, y, :, pl.ds(rank, rank)], lsem.at[1]),
        pltpu.make_async_copy(k_hbm, k_vm, lsem.at[2]),
        pltpu.make_async_copy(d_hbm, d_vm, lsem.at[3]),
    ]
    for load in loads:
        load.start()
    barrier = pltpu.get_barrier_semaphore()
    for peer in everyone:
        pl.semaphore_signal(barrier, inc=1, device_id=peer, device_id_type=pl.DeviceIdType.MESH)
    pl.semaphore_wait(barrier, len(everyone))
    loads[0].wait()
    loads[1].wait()

    chunk = a_buf.at[z, y]
    along = [remote(chunk, chunk, peer) for peer in zpeers]
    across = [remote(chunk, chunk, ypeer)]

    loads[2].wait()
    loads[3].wait()
    for part in range(2):
        xt[:, :, :, part * rows:(part + 1) * rows] = regroup(k_vm[part].T, (nz, 2, own, rows))
    for step in range(nz - 1):
        along[step].wait_recv()
        origin = lax.rem(z - step - 1 + nz, nz)
        chunk = a_buf.at[origin, y]
        across.append(remote(chunk, chunk, ypeer))
    for part in range(2):
        xt[:, :, :, (part + 2) * rows:(part + 3) * rows] = regroup(d_vm[part].T, (nz, 2, own, rows))
    for copy in across:
        copy.wait_recv()

    a = regroup(a_buf[...], (cols, 2 * rank))
    b = jnp.concatenate([-a[:, rank:], a[:, :rank]], axis=1)

    def products(h):
        at = pl.ds(pl.multiple_of(h * half, half), half)
        first = dot(jnp.concatenate([k_vm[0, at, :], d_vm[0, at, :]], axis=0), a)
        second = dot(jnp.concatenate([k_vm[1, at, :], d_vm[1, at, :]], axis=0), b)
        return first[:half] + second[:half], first[half:] - second[half:]

    g_loc[...] = gram(a).reshape(2, ghalf, 2 * rank)
    g_core = remote(g_loc.at[1 - c], g_rx, cpeer)
    z_other, v_other = products(1 - c)
    c_tx[0] = z_other
    c_tx[1] = v_other
    zv_core = remote(c_tx, c_rx, cpeer)
    g_core.wait_recv()
    g_pair = g_loc[c] + g_rx[...]
    g_xtx[...] = g_pair
    g_across = [remote(g_xtx, g_xrx.at[i], peer) for i, peer in enumerate(xpeers)]
    z_own, v_own = products(c)
    zv_core.wait_recv()
    z_own = z_own + c_rx[0]
    v_own = v_own + c_rx[1]
    z_xtx[...] = z_own
    z_across = [remote(z_xtx, z_xrx.at[i], peer) for i, peer in enumerate(xpeers)]
    v_xtx[...] = v_own.astype(BF16)
    v_across = [remote(v_xtx, v_xrx.at[i], peer) for i, peer in enumerate(xpeers)]
    for i, copy in enumerate(g_across):
        copy.wait_recv()
        g_pair = g_pair + g_xrx[i]
    g_fin[c] = g_pair
    g_back = remote(g_fin.at[c], g_fin.at[c], cpeer)
    g_back.wait_recv()
    g_high, g_low = complex_right(g_fin[...].reshape(rank, 2 * rank))
    for i, copy in enumerate(z_across):
        copy.wait_recv()
        z_own = z_own + z_xrx[i]
    z_round = z_own.astype(BF16)
    w_own = dot(z_round, g_high) + dot(z_round, g_low)
    for i, copy in enumerate(v_across):
        copy.wait_recv()
        v_own = v_own + v_xrx[i].astype(F32)
    w_own = jnp.concatenate(
        [w_own[:, :rank] - v_own[:, :rank], w_own[:, rank:] + v_own[:, rank:]], axis=1
    ).astype(BF16)
    zw[c] = jnp.concatenate([z_round, w_own], axis=1)
    zw_core = remote(zw.at[c], zw.at[c], cpeer)
    zw_core.wait_recv()

    full = zw[...].reshape(rows, 4 * rank)
    zr, zi, wr, wi = (full[:, i * rank:(i + 1) * rank] for i in range(4))
    h_high, h_low = complex_right(gram(full[:, :2 * rank]))
    right = jnp.concatenate(
        [
            jnp.concatenate([wr, wi], axis=1),
            jnp.concatenate([wi, -wr], axis=1),
            jnp.concatenate([-zr, zi], axis=1),
            jnp.concatenate([-zi, -zr], axis=1),
        ],
        axis=0,
    )

    def gradient(side):
        left = regroup(xt[:, side], (nz * own, 4 * rows))
        q_side = regroup(a_buf[:, side], (nz * own, 2 * rank))
        total = dot(left, right) + dot(q_side, h_high) + dot(q_side, h_low)
        return total.reshape(nz, own, 2 * rank)

    y_tx[...] = gradient(1 - y).astype(BF16)
    to_y = {}
    order = list(range(1, nz)) + [0]
    for d in order:
        at = lax.rem(z + d, nz)
        to_y[d] = remote(y_tx.at[at], y_rx.at[at], ypeer)
    t_tx[...] = gradient(y)
    to_z = []
    for d in order:
        at = lax.rem(z + d, nz)
        to_y[d].wait_recv()
        mine = t_tx[at] + y_rx[at].astype(F32)
        if d:
            t_rx[1, d - 1] = mine.astype(BF16)
            to_z.append(remote(t_rx.at[1, d - 1], t_rx.at[0, d - 1], zpeers[d - 1]))
    for i, copy in enumerate(to_z):
        copy.wait_recv()
        mine = mine + t_rx[0, i].astype(F32)
    mine = mine * scaling
    o_ref[0, 0] = mine[:, :rank]
    o_ref[1, 0] = mine[:, rank:]
    for copy in started:
        copy.wait_send()


def body(nr, ns, k_op, data, factor):
    rows, cols = k_op.shape[1:]
    own, rank = factor.shape[2:]
    nz, nx = nr // 2, ns // 2
    half = rows // 2
    count = 2 * (nz - 1) + 1 + 1 + 2 + 3 * (nx - 1) + 2 + nz + (nz - 1) + 4
    slots = max(nx - 1, 1)
    scratch = [
        pltpu.VMEM((nz, 2, own, 2 * rank), BF16),
        pltpu.VMEM((2, rows, cols), BF16),
        pltpu.VMEM((2, rows, cols), BF16),
        pltpu.VMEM((nz, 2, own, 4 * rows), BF16),
        pltpu.VMEM((2, rank // 2, 2 * rank), F32),
        pltpu.VMEM((rank // 2, 2 * rank), F32),
        pltpu.VMEM((rank // 2, 2 * rank), F32),
        pltpu.VMEM((slots, rank // 2, 2 * rank), F32),
        pltpu.VMEM((2, rank // 2, 2 * rank), F32),
        pltpu.VMEM((2, half, 2 * rank), F32),
        pltpu.VMEM((2, half, 2 * rank), F32),
        pltpu.VMEM((half, 2 * rank), F32),
        pltpu.VMEM((slots, half, 2 * rank), F32),
        pltpu.VMEM((half, 2 * rank), BF16),
        pltpu.VMEM((slots, half, 2 * rank), BF16),
        pltpu.VMEM((2, half, 4 * rank), BF16),
        pltpu.VMEM((nz, own, 2 * rank), BF16),
        pltpu.VMEM((nz, own, 2 * rank), BF16),
        pltpu.VMEM((nz, own, 2 * rank), F32),
        pltpu.VMEM((2, max(nz - 1, 1), own, 2 * rank), BF16),
        pltpu.SemaphoreType.DMA((4,)),
        pltpu.SemaphoreType.DMA((count,)),
        pltpu.SemaphoreType.DMA((count,)),
    ]
    scaling = 1.0 / math.sqrt(rows * nr)
    return pl.pallas_call(
        functools.partial(kernel, nz, nx, scaling),
        out_shape=jax.ShapeDtypeStruct((2, 1, own, rank), F32),
        in_specs=[pl.BlockSpec(memory_space=pl.ANY)] * 3,
        out_specs=pl.BlockSpec(memory_space=pltpu.VMEM),
        scratch_shapes=scratch,
        compiler_params=pltpu.CompilerParams(
            collective_id=0, has_side_effects=True, vmem_limit_bytes=56 * 1024 * 1024
        ),
        name="gradient",
    )(k_op, data, factor)


def solution(mesh):
    return jax.shard_map(
        functools.partial(body, mesh.shape["rcv"], mesh.shape["src"]),
        mesh=mesh,
        in_specs=(P(None, "rcv", "src"), P(None, "rcv", "src"), P(None, "src", "rcv", None)),
        out_specs=P(None, "src", "rcv", None),
        check_vma=False,
    )
```

```python
import functools
import math

import jax
import jax.numpy as jnp
from jax import lax
from jax.experimental import pallas as pl
from jax.experimental.pallas import tpu as pltpu
from jax.sharding import PartitionSpec as P

F32 = jnp.float32
BF16 = jnp.bfloat16


def dot(left, right):
    return jnp.dot(left, right, preferred_element_type=F32)


def gram(cat):
    rank = cat.shape[1] // 2
    full = lax.dot_general(cat, cat, (((0,), (0,)), ((), ())), preferred_element_type=F32)
    real = full[:rank, :rank] + full[rank:, rank:]
    imaginary = full[rank:, :rank] - full[:rank, rank:]
    return jnp.concatenate([real, imaginary], axis=1)


def complex_right(cat):
    rank = cat.shape[1] // 2
    real, imaginary = cat[:, :rank], cat[:, rank:]
    full = jnp.concatenate([cat, jnp.concatenate([-imaginary, real], axis=1)], axis=0)
    high = full.astype(BF16)
    low = (full - high.astype(F32)).astype(BF16)
    return high, low


def regroup(values, shape):
    if shape[-2] % 16 == 0 and values.shape[-2] % 16 == 0:
        return values.reshape(shape)
    return values.astype(F32).reshape(shape).astype(BF16)


def kernel(
    nz, nx, scaling,
    k_hbm, d_hbm, q_hbm, o_ref,
    a_buf, k_vm, d_vm, xt,
    g_loc, g_rx, g_xtx, g_xrx, g_ytx, g_yrx, g_fin,
    c_tx, c_rx, z_xtx, z_xrx, v_xtx, v_xrx, z_all, w_all,
    y_tx, y_rx, total, t_tx, t_rx,
    lsem, ssem, rsem, zsend, zrecv,
):
    rcv, src = lax.axis_index("rcv"), lax.axis_index("src")
    z, y = rcv // 2, rcv % 2
    x, c = src // 2, src % 2
    ypeer = {"rcv": z * 2 + 1 - y}
    cpeer = {"src": x * 2 + 1 - c}
    low = z < nz // 2
    far = []
    for step in range(nz - 1):
        down, up = nz - 1 - step, step
        down = jnp.where(down <= z, down - 1, down)
        up = jnp.where(up >= z, up + 1, up)
        far.append(jnp.where(low, down, up))
    zpeers = [{"rcv": other * 2 + y} for other in far]
    xpeers = [{"src": lax.rem(x + d, nx) * 2 + c} for d in range(1, nx)]
    everyone = [ypeer, cpeer] + zpeers + xpeers
    rows, cols = k_vm.shape[1], k_vm.shape[2]
    half = rows // 2
    rank = q_hbm.shape[3]
    own = q_hbm.shape[2]
    ghalf = rank // 2

    counter = [0]
    started = []

    def remote(source, target, peer):
        at = counter[0]
        counter[0] += 1
        copy = pltpu.make_async_remote_copy(
            src_ref=source, dst_ref=target, send_sem=ssem.at[at], recv_sem=rsem.at[at],
            device_id=peer, device_id_type=pl.DeviceIdType.MESH,
        )
        copy.start()
        started.append(copy)
        return copy

    def along_z(phase, source, target, other):
        copy = pltpu.make_async_remote_copy(
            src_ref=source, dst_ref=target,
            send_sem=zsend.at[phase, other], recv_sem=zrecv.at[phase, z],
            device_id={"rcv": other * 2 + y}, device_id_type=pl.DeviceIdType.MESH,
        )
        copy.start()
        started.append(copy)

    def from_z(phase, target, other):
        pltpu.make_async_remote_copy(
            src_ref=target, dst_ref=target,
            send_sem=zsend.at[phase, other], recv_sem=zrecv.at[phase, other],
            device_id={"rcv": other * 2 + y}, device_id_type=pl.DeviceIdType.MESH,
        ).wait_recv()

    loads = [
        pltpu.make_async_copy(q_hbm.at[0, 0], a_buf.at[z, y, :, pl.ds(0, rank)], lsem.at[0]),
        pltpu.make_async_copy(q_hbm.at[1, 0], a_buf.at[z, y, :, pl.ds(rank, rank)], lsem.at[1]),
        pltpu.make_async_copy(k_hbm, k_vm, lsem.at[2]),
        pltpu.make_async_copy(d_hbm, d_vm, lsem.at[3]),
    ]
    for load in loads:
        load.start()
    barrier = pltpu.get_barrier_semaphore()
    for peer in everyone:
        pl.semaphore_signal(barrier, inc=1, device_id=peer, device_id_type=pl.DeviceIdType.MESH)
    pl.semaphore_wait(barrier, len(everyone))
    loads[0].wait()
    loads[1].wait()

    chunk = a_buf.at[z, y]
    for other in far:
        along_z(0, chunk, chunk, other)
    across = [remote(chunk, chunk, ypeer)]
    for other in far[::-1]:
        chunk = a_buf.at[other, y]
        from_z(0, chunk, other)
        across.append(remote(chunk, chunk, ypeer))

    g_loc[...] = gram(regroup(a_buf[:, y], (nz * own, 2 * rank))).reshape(2, ghalf, 2 * rank)
    g_core = remote(g_loc.at[1 - c], g_rx, cpeer)
    g_core.wait_recv()
    g_pair = g_loc[c] + g_rx[...]
    g_xtx[...] = g_pair
    g_across = [remote(g_xtx, g_xrx.at[i], peer) for i, peer in enumerate(xpeers)]

    for copy in across:
        copy.wait_recv()
    a = regroup(a_buf[...], (cols, 2 * rank))
    b = jnp.concatenate([-a[:, rank:], a[:, :rank]], axis=1)
    loads[2].wait()
    loads[3].wait()

    def product(ref, h, sign):
        at = pl.ds(pl.multiple_of(h * half, half), half)
        return dot(ref[0, at, :], a) + sign * dot(ref[1, at, :], b)

    c_tx[0] = product(k_vm, 1 - c, 1.0)
    z_core = remote(c_tx.at[0], c_rx.at[0], cpeer)
    z_own = product(k_vm, c, 1.0)
    c_tx[1] = product(d_vm, 1 - c, -1.0)
    v_core = remote(c_tx.at[1], c_rx.at[1], cpeer)
    z_core.wait_recv()
    z_own = z_own + c_rx[0]
    z_xtx[...] = z_own
    z_across = [remote(z_xtx, z_xrx.at[i], peer) for i, peer in enumerate(xpeers)]
    v_own = product(d_vm, c, -1.0)
    v_core.wait_recv()
    v_own = v_own + c_rx[1]
    v_xtx[...] = v_own.astype(BF16)
    v_across = [remote(v_xtx, v_xrx.at[i], peer) for i, peer in enumerate(xpeers)]
    for part in range(2):
        xt[:, :, :, part * rows:(part + 1) * rows] = regroup(k_vm[part].T, (nz, 2, own, rows))
        xt[:, :, :, (part + 2) * rows:(part + 3) * rows] = regroup(d_vm[part].T, (nz, 2, own, rows))
    for i, copy in enumerate(g_across):
        copy.wait_recv()
        g_pair = g_pair + g_xrx[i]
    g_ytx[...] = g_pair
    g_side = remote(g_ytx, g_yrx, ypeer)
    g_side.wait_recv()
    g_fin[c] = g_pair + g_yrx[...]
    g_back = remote(g_fin.at[c], g_fin.at[c], cpeer)
    g_back.wait_recv()
    g_high, g_low = complex_right(g_fin[...].reshape(rank, 2 * rank))
    for i, copy in enumerate(z_across):
        copy.wait_recv()
        z_own = z_own + z_xrx[i]
    z_round = z_own.astype(BF16)
    z_all[c] = z_round
    z_back = remote(z_all.at[c], z_all.at[c], cpeer)
    w_own = dot(z_round, g_high) + dot(z_round, g_low)
    z_back.wait_recv()

    z_cat = z_all[...].reshape(rows, 2 * rank)
    zr, zi = z_cat[:, :rank], z_cat[:, rank:]
    h_high, h_low = complex_right(gram(z_cat))
    z_right = jnp.concatenate(
        [jnp.concatenate([-zr, zi], axis=1), jnp.concatenate([-zi, -zr], axis=1)], axis=0
    )
    for side in range(2):
        left = regroup(xt[:, side, :, 2 * rows:], (nz * own, 2 * rows))
        q_side = regroup(a_buf[:, side], (nz * own, 2 * rank))
        total[side] = dot(left, z_right) + dot(q_side, h_high) + dot(q_side, h_low)

    for i, copy in enumerate(v_across):
        copy.wait_recv()
        v_own = v_own + v_xrx[i].astype(F32)
    w_all[c] = jnp.concatenate(
        [w_own[:, :rank] - v_own[:, :rank], w_own[:, rank:] + v_own[:, rank:]], axis=1
    ).astype(BF16)
    w_back = remote(w_all.at[c], w_all.at[c], cpeer)
    w_back.wait_recv()
    w_cat = w_all[...].reshape(rows, 2 * rank)
    wr, wi = w_cat[:, :rank], w_cat[:, rank:]
    w_right = jnp.concatenate([w_cat, jnp.concatenate([wi, -wr], axis=1)], axis=0)

    def gradient(side):
        left = regroup(xt[:, side, :, :2 * rows], (nz * own, 2 * rows))
        return (total[side] + dot(left, w_right)).reshape(nz, own, 2 * rank)

    y_tx[...] = gradient(1 - y).astype(BF16)
    to_y = [remote(y_tx.at[at], y_rx.at[at], ypeer) for at in far + [z]]
    t_tx[...] = gradient(y)
    for at, copy in zip(far, to_y):
        copy.wait_recv()
        t_rx[1, at] = (t_tx[at] + y_rx[at].astype(F32)).astype(BF16)
        along_z(1, t_rx.at[1, at], t_rx.at[0, z], at)
    to_y[-1].wait_recv()
    mine = t_tx[z] + y_rx[z].astype(F32)
    for other in far[::-1]:
        from_z(1, t_rx.at[0, other], other)
        mine = mine + t_rx[0, other].astype(F32)
    mine = mine * scaling
    o_ref[0, 0] = mine[:, :rank]
    o_ref[1, 0] = mine[:, rank:]
    for copy in started:
        copy.wait_send()


def body(nr, ns, k_op, data, factor):
    rows, cols = k_op.shape[1:]
    own, rank = factor.shape[2:]
    nz, nx = nr // 2, ns // 2
    half = rows // 2
    count = 2 * nz + 3 * (nx - 1) + 7
    slots = max(nx - 1, 1)
    scratch = [
        pltpu.VMEM((nz, 2, own, 2 * rank), BF16),
        pltpu.VMEM((2, rows, cols), BF16),
        pltpu.VMEM((2, rows, cols), BF16),
        pltpu.VMEM((nz, 2, own, 4 * rows), BF16),
        pltpu.VMEM((2, rank // 2, 2 * rank), F32),
        pltpu.VMEM((rank // 2, 2 * rank), F32),
        pltpu.VMEM((rank // 2, 2 * rank), F32),
        pltpu.VMEM((slots, rank // 2, 2 * rank), F32),
        pltpu.VMEM((rank // 2, 2 * rank), F32),
        pltpu.VMEM((rank // 2, 2 * rank), F32),
        pltpu.VMEM((2, rank // 2, 2 * rank), F32),
        pltpu.VMEM((2, half, 2 * rank), F32),
        pltpu.VMEM((2, half, 2 * rank), F32),
        pltpu.VMEM((half, 2 * rank), F32),
        pltpu.VMEM((slots, half, 2 * rank), F32),
        pltpu.VMEM((half, 2 * rank), BF16),
        pltpu.VMEM((slots, half, 2 * rank), BF16),
        pltpu.VMEM((2, half, 2 * rank), BF16),
        pltpu.VMEM((2, half, 2 * rank), BF16),
        pltpu.VMEM((nz, own, 2 * rank), BF16),
        pltpu.VMEM((nz, own, 2 * rank), BF16),
        pltpu.VMEM((2, nz * own, 2 * rank), F32),
        pltpu.VMEM((nz, own, 2 * rank), F32),
        pltpu.VMEM((2, nz, own, 2 * rank), BF16),
        pltpu.SemaphoreType.DMA((4,)),
        pltpu.SemaphoreType.DMA((count,)),
        pltpu.SemaphoreType.DMA((count,)),
        pltpu.SemaphoreType.DMA((2, nz)),
        pltpu.SemaphoreType.DMA((2, nz)),
    ]
    scaling = 1.0 / math.sqrt(rows * nr)
    return pl.pallas_call(
        functools.partial(kernel, nz, nx, scaling),
        out_shape=jax.ShapeDtypeStruct((2, 1, own, rank), F32),
        in_specs=[pl.BlockSpec(memory_space=pl.ANY)] * 3,
        out_specs=pl.BlockSpec(memory_space=pltpu.VMEM),
        scratch_shapes=scratch,
        compiler_params=pltpu.CompilerParams(
            collective_id=0, has_side_effects=True, vmem_limit_bytes=56 * 1024 * 1024
        ),
        name="gradient",
    )(k_op, data, factor)


def solution(mesh):
    return jax.shard_map(
        functools.partial(body, mesh.shape["rcv"], mesh.shape["src"]),
        mesh=mesh,
        in_specs=(P(None, "rcv", "src"), P(None, "rcv", "src"), P(None, "src", "rcv", None)),
        out_specs=P(None, "src", "rcv", None),
        check_vma=False,
    )
```

```python
import functools
import math

import jax
import jax.numpy as jnp
from jax import lax
from jax.experimental import pallas as pl
from jax.experimental.pallas import tpu as pltpu
from jax.sharding import PartitionSpec as P

F32 = jnp.float32
BF16 = jnp.bfloat16


def dot(left, right):
    return jnp.dot(left, right, preferred_element_type=F32)


def gram(cat):
    rank = cat.shape[1] // 2
    full = lax.dot_general(cat, cat, (((0,), (0,)), ((), ())), preferred_element_type=F32)
    real = full[:rank, :rank] + full[rank:, rank:]
    imaginary = full[rank:, :rank] - full[:rank, rank:]
    return jnp.concatenate([real, imaginary], axis=1)


def complex_right(cat):
    rank = cat.shape[1] // 2
    real, imaginary = cat[:, :rank], cat[:, rank:]
    full = jnp.concatenate([cat, jnp.concatenate([-imaginary, real], axis=1)], axis=0)
    high = full.astype(BF16)
    low = (full - high.astype(F32)).astype(BF16)
    return high, low


def regroup(values, shape):
    if shape[-2] % 16 == 0 and values.shape[-2] % 16 == 0:
        return values.reshape(shape)
    return values.astype(F32).reshape(shape).astype(BF16)


def kernel(
    nz, nx, scaling,
    k_hbm, d_hbm, q_hbm, o_ref,
    a_buf, k_vm, d_vm, xt,
    g_loc, g_rx, g_xtx, g_xrx, g_ytx, g_yrx, g_fin,
    c_tx, c_rx, z_xtx, z_xrx, v_xtx, v_xrx, z_all, w_all,
    y_tx, y_rx, total, t_tx, t_rx,
    lsem, ssem, rsem, zsend, zrecv, upper, lower,
):
    rcv, src = lax.axis_index("rcv"), lax.axis_index("src")
    z, y = rcv // 2, rcv % 2
    x, c = src // 2, src % 2
    ypeer = {"rcv": z * 2 + 1 - y}
    cpeer = {"src": x * 2 + 1 - c}
    low = z < nz // 2
    far = []
    for step in range(nz - 1):
        down, up = nz - 1 - step, step
        down = jnp.where(down <= z, down - 1, down)
        up = jnp.where(up >= z, up + 1, up)
        far.append(jnp.where(low, down, up))
    xpeers = [{"src": lax.rem(x + d, nx) * 2 + c} for d in range(1, nx)]
    near = [ypeer, cpeer] + xpeers
    rows, cols = k_vm.shape[1], k_vm.shape[2]
    half = rows // 2
    rank = q_hbm.shape[3]
    own = q_hbm.shape[2]
    ghalf = rank // 2

    counter = [0]
    started = []

    def remote(source, target, peer):
        at = counter[0]
        counter[0] += 1
        copy = pltpu.make_async_remote_copy(
            src_ref=source, dst_ref=target, send_sem=ssem.at[at], recv_sem=rsem.at[at],
            device_id=peer, device_id_type=pl.DeviceIdType.MESH,
        )
        copy.start()
        started.append(copy)
        return copy

    def along_z(phase, source, target, other):
        copy = pltpu.make_async_remote_copy(
            src_ref=source, dst_ref=target,
            send_sem=zsend.at[phase, other], recv_sem=zrecv.at[phase, z],
            device_id={"rcv": other * 2 + y}, device_id_type=pl.DeviceIdType.MESH,
        )
        copy.start()

    def from_z(phase, target, other):
        pltpu.make_async_remote_copy(
            src_ref=target, dst_ref=target,
            send_sem=zsend.at[phase, other], recv_sem=zrecv.at[phase, other],
            device_id={"rcv": other * 2 + y}, device_id_type=pl.DeviceIdType.MESH,
        ).wait_recv()

    loads = [
        pltpu.make_async_copy(q_hbm.at[0, 0], a_buf.at[z, y, :, pl.ds(0, rank)], lsem.at[0]),
        pltpu.make_async_copy(q_hbm.at[1, 0], a_buf.at[z, y, :, pl.ds(rank, rank)], lsem.at[1]),
        pltpu.make_async_copy(k_hbm, k_vm, lsem.at[2]),
        pltpu.make_async_copy(d_hbm, d_vm, lsem.at[3]),
    ]
    for load in loads:
        load.start()
    barrier = pltpu.get_barrier_semaphore()
    for peer in near:
        pl.semaphore_signal(barrier, inc=1, device_id=peer, device_id_type=pl.DeviceIdType.MESH)

    def signal_z(semaphore, other):
        pl.semaphore_signal(
            semaphore, inc=1, device_id={"rcv": other * 2 + y}, device_id_type=pl.DeviceIdType.MESH
        )

    @pl.when(z > 0)
    def _():
        signal_z(barrier, z - 1)

    @pl.when(z < nz - 1)
    def _():
        signal_z(barrier, z + 1)

    beside = jnp.where(z > 0, 1, 0) + jnp.where(z < nz - 1, 1, 0)
    pl.semaphore_wait(barrier, len(near) + beside)

    def tell(k):
        @pl.when((z > 0) & (z + k < nz))
        def _():
            signal_z(upper.at[k - 1], z - 1)

        @pl.when((z < nz - 1) & (z - k >= 0))
        def _():
            signal_z(lower.at[k - 1], z + 1)

    if nz > 2:
        tell(1)
    loads[0].wait()
    loads[1].wait()

    chunk = a_buf.at[z, y]
    across = [remote(chunk, chunk, ypeer)]
    for k in range(1, nz):
        @pl.when(z + k < nz)
        def _():
            if k > 1:
                pl.semaphore_wait(upper.at[k - 2], 1)
            along_z(0, chunk, chunk, z + k)

        @pl.when(z - k >= 0)
        def _():
            if k > 1:
                pl.semaphore_wait(lower.at[k - 2], 1)
            along_z(0, chunk, chunk, z - k)

        if 1 < k < nz - 1:
            tell(k)
    for other in far[::-1]:
        chunk = a_buf.at[other, y]
        from_z(0, chunk, other)
        across.append(remote(chunk, chunk, ypeer))

    g_loc[...] = gram(regroup(a_buf[:, y], (nz * own, 2 * rank))).reshape(2, ghalf, 2 * rank)
    g_core = remote(g_loc.at[1 - c], g_rx, cpeer)
    g_core.wait_recv()
    g_pair = g_loc[c] + g_rx[...]
    g_xtx[...] = g_pair
    g_across = [remote(g_xtx, g_xrx.at[i], peer) for i, peer in enumerate(xpeers)]

    for copy in across:
        copy.wait_recv()
    a = regroup(a_buf[...], (cols, 2 * rank))
    b = jnp.concatenate([-a[:, rank:], a[:, :rank]], axis=1)
    loads[2].wait()
    loads[3].wait()

    def product(ref, h, sign):
        at = pl.ds(pl.multiple_of(h * half, half), half)
        return dot(ref[0, at, :], a) + sign * dot(ref[1, at, :], b)

    c_tx[0] = product(k_vm, 1 - c, 1.0)
    z_core = remote(c_tx.at[0], c_rx.at[0], cpeer)
    z_own = product(k_vm, c, 1.0)
    c_tx[1] = product(d_vm, 1 - c, -1.0)
    v_core = remote(c_tx.at[1], c_rx.at[1], cpeer)
    z_core.wait_recv()
    z_own = z_own + c_rx[0]
    z_xtx[...] = z_own
    z_across = [remote(z_xtx, z_xrx.at[i], peer) for i, peer in enumerate(xpeers)]
    v_own = product(d_vm, c, -1.0)
    v_core.wait_recv()
    v_own = v_own + c_rx[1]
    v_xtx[...] = v_own.astype(BF16)
    v_across = [remote(v_xtx, v_xrx.at[i], peer) for i, peer in enumerate(xpeers)]
    for part in range(2):
        xt[:, :, :, part * rows:(part + 1) * rows] = regroup(k_vm[part].T, (nz, 2, own, rows))
        xt[:, :, :, (part + 2) * rows:(part + 3) * rows] = regroup(d_vm[part].T, (nz, 2, own, rows))
    for i, copy in enumerate(g_across):
        copy.wait_recv()
        g_pair = g_pair + g_xrx[i]
    g_ytx[...] = g_pair
    g_side = remote(g_ytx, g_yrx, ypeer)
    g_side.wait_recv()
    g_fin[c] = g_pair + g_yrx[...]
    g_back = remote(g_fin.at[c], g_fin.at[c], cpeer)
    g_back.wait_recv()
    g_high, g_low = complex_right(g_fin[...].reshape(rank, 2 * rank))
    for i, copy in enumerate(z_across):
        copy.wait_recv()
        z_own = z_own + z_xrx[i]
    z_round = z_own.astype(BF16)
    z_all[c] = z_round
    z_back = remote(z_all.at[c], z_all.at[c], cpeer)
    w_own = dot(z_round, g_high) + dot(z_round, g_low)
    z_back.wait_recv()

    z_cat = z_all[...].reshape(rows, 2 * rank)
    zr, zi = z_cat[:, :rank], z_cat[:, rank:]
    h_high, h_low = complex_right(gram(z_cat))
    z_right = jnp.concatenate(
        [jnp.concatenate([-zr, zi], axis=1), jnp.concatenate([-zi, -zr], axis=1)], axis=0
    )
    for side in range(2):
        left = regroup(xt[:, side, :, 2 * rows:], (nz * own, 2 * rows))
        q_side = regroup(a_buf[:, side], (nz * own, 2 * rank))
        total[side] = dot(left, z_right) + dot(q_side, h_high) + dot(q_side, h_low)

    for i, copy in enumerate(v_across):
        copy.wait_recv()
        v_own = v_own + v_xrx[i].astype(F32)
    w_all[c] = jnp.concatenate(
        [w_own[:, :rank] - v_own[:, :rank], w_own[:, rank:] + v_own[:, rank:]], axis=1
    ).astype(BF16)
    w_back = remote(w_all.at[c], w_all.at[c], cpeer)
    w_back.wait_recv()
    w_cat = w_all[...].reshape(rows, 2 * rank)
    wr, wi = w_cat[:, :rank], w_cat[:, rank:]
    w_right = jnp.concatenate([w_cat, jnp.concatenate([wi, -wr], axis=1)], axis=0)

    def gradient(side):
        left = regroup(xt[:, side, :, :2 * rows], (nz * own, 2 * rows))
        return (total[side] + dot(left, w_right)).reshape(nz, own, 2 * rank)

    y_tx[...] = gradient(1 - y).astype(BF16)
    to_y = [remote(y_tx.at[at], y_rx.at[at], ypeer) for at in far + [z]]
    t_tx[...] = gradient(y)
    for at, copy in zip(far, to_y):
        copy.wait_recv()
        t_rx[1, at] = (t_tx[at] + y_rx[at].astype(F32)).astype(BF16)
        along_z(1, t_rx.at[1, at], t_rx.at[0, z], at)
    to_y[-1].wait_recv()
    mine = t_tx[z] + y_rx[z].astype(F32)
    for other in far[::-1]:
        from_z(1, t_rx.at[0, other], other)
        mine = mine + t_rx[0, other].astype(F32)
    mine = mine * scaling
    o_ref[0, 0] = mine[:, :rank]
    o_ref[1, 0] = mine[:, rank:]
    for copy in started:
        copy.wait_send()
    for other in far:
        for phase, sent in enumerate((a_buf.at[z, y], t_rx.at[1, other])):
            pltpu.make_async_remote_copy(
                src_ref=sent, dst_ref=sent,
                send_sem=zsend.at[phase, other], recv_sem=zrecv.at[phase, other],
                device_id={"rcv": other * 2 + y}, device_id_type=pl.DeviceIdType.MESH,
            ).wait_send()


def body(nr, ns, k_op, data, factor):
    rows, cols = k_op.shape[1:]
    own, rank = factor.shape[2:]
    nz, nx = nr // 2, ns // 2
    half = rows // 2
    count = 2 * nz + 3 * (nx - 1) + 7
    slots = max(nx - 1, 1)
    scratch = [
        pltpu.VMEM((nz, 2, own, 2 * rank), BF16),
        pltpu.VMEM((2, rows, cols), BF16),
        pltpu.VMEM((2, rows, cols), BF16),
        pltpu.VMEM((nz, 2, own, 4 * rows), BF16),
        pltpu.VMEM((2, rank // 2, 2 * rank), F32),
        pltpu.VMEM((rank // 2, 2 * rank), F32),
        pltpu.VMEM((rank // 2, 2 * rank), F32),
        pltpu.VMEM((slots, rank // 2, 2 * rank), F32),
        pltpu.VMEM((rank // 2, 2 * rank), F32),
        pltpu.VMEM((rank // 2, 2 * rank), F32),
        pltpu.VMEM((2, rank // 2, 2 * rank), F32),
        pltpu.VMEM((2, half, 2 * rank), F32),
        pltpu.VMEM((2, half, 2 * rank), F32),
        pltpu.VMEM((half, 2 * rank), F32),
        pltpu.VMEM((slots, half, 2 * rank), F32),
        pltpu.VMEM((half, 2 * rank), BF16),
        pltpu.VMEM((slots, half, 2 * rank), BF16),
        pltpu.VMEM((2, half, 2 * rank), BF16),
        pltpu.VMEM((2, half, 2 * rank), BF16),
        pltpu.VMEM((nz, own, 2 * rank), BF16),
        pltpu.VMEM((nz, own, 2 * rank), BF16),
        pltpu.VMEM((2, nz * own, 2 * rank), F32),
        pltpu.VMEM((nz, own, 2 * rank), F32),
        pltpu.VMEM((2, nz, own, 2 * rank), BF16),
        pltpu.SemaphoreType.DMA((4,)),
        pltpu.SemaphoreType.DMA((count,)),
        pltpu.SemaphoreType.DMA((count,)),
        pltpu.SemaphoreType.DMA((2, nz)),
        pltpu.SemaphoreType.DMA((2, nz)),
        pltpu.SemaphoreType.REGULAR((nz,)),
        pltpu.SemaphoreType.REGULAR((nz,)),
    ]
    scaling = 1.0 / math.sqrt(rows * nr)
    return pl.pallas_call(
        functools.partial(kernel, nz, nx, scaling),
        out_shape=jax.ShapeDtypeStruct((2, 1, own, rank), F32),
        in_specs=[pl.BlockSpec(memory_space=pl.ANY)] * 3,
        out_specs=pl.BlockSpec(memory_space=pltpu.VMEM),
        scratch_shapes=scratch,
        compiler_params=pltpu.CompilerParams(
            collective_id=0, has_side_effects=True, vmem_limit_bytes=56 * 1024 * 1024
        ),
        name="gradient",
    )(k_op, data, factor)


def solution(mesh):
    return jax.shard_map(
        functools.partial(body, mesh.shape["rcv"], mesh.shape["src"]),
        mesh=mesh,
        in_specs=(P(None, "rcv", "src"), P(None, "rcv", "src"), P(None, "src", "rcv", None)),
        out_specs=P(None, "src", "rcv", None),
        check_vma=False,
    )
```

```python
import functools
import math

import jax
import jax.numpy as jnp
from jax import lax
from jax.experimental import pallas as pl
from jax.experimental.pallas import tpu as pltpu
from jax.sharding import PartitionSpec as P

F32 = jnp.float32
BF16 = jnp.bfloat16


def dot(left, right):
    return jnp.dot(left, right, preferred_element_type=F32)


def gram(cat):
    rank = cat.shape[1] // 2
    full = lax.dot_general(cat, cat, (((0,), (0,)), ((), ())), preferred_element_type=F32)
    real = full[:rank, :rank] + full[rank:, rank:]
    imaginary = full[rank:, :rank] - full[:rank, rank:]
    return jnp.concatenate([real, imaginary], axis=1)


def complex_right(cat):
    rank = cat.shape[1] // 2
    real, imaginary = cat[:, :rank], cat[:, rank:]
    full = jnp.concatenate([cat, jnp.concatenate([-imaginary, real], axis=1)], axis=0)
    high = full.astype(BF16)
    low = (full - high.astype(F32)).astype(BF16)
    return high, low


def regroup(values, shape):
    if shape[-2] % 16 == 0 and values.shape[-2] % 16 == 0:
        return values.reshape(shape)
    return values.astype(F32).reshape(shape).astype(BF16)


def kernel(
    nz, nx, scaling,
    k_hbm, d_hbm, q_hbm, o_ref,
    a_buf, k_vm, d_vm, xt,
    g_loc, g_rx, g_xtx, g_xrx, g_ytx, g_yrx, g_fin,
    c_tx, c_rx, z_xtx, z_xrx, v_xtx, v_xrx, z_all, w_all,
    y_tx, y_rx, total, t_tx, t_rx,
    lsem, ssem, rsem, zsend, zrecv, upper, lower,
):
    rcv, src = lax.axis_index("rcv"), lax.axis_index("src")
    z, y = rcv // 2, rcv % 2
    x, c = src // 2, src % 2
    ypeer = {"rcv": z * 2 + 1 - y}
    cpeer = {"src": x * 2 + 1 - c}
    low = z < nz // 2
    far = []
    for step in range(nz - 1):
        down, up = nz - 1 - step, step
        down = jnp.where(down <= z, down - 1, down)
        up = jnp.where(up >= z, up + 1, up)
        far.append(jnp.where(low, down, up))
    xpeers = [{"src": lax.rem(x + d, nx) * 2 + c} for d in range(1, nx)]
    near = [ypeer, cpeer] + xpeers
    rows, cols = k_vm.shape[1], k_vm.shape[2]
    half = rows // 2
    rank = q_hbm.shape[3]
    own = q_hbm.shape[2]
    ghalf = rank // 2

    counter = [0]
    started = []

    def remote(source, target, peer):
        at = counter[0]
        counter[0] += 1
        copy = pltpu.make_async_remote_copy(
            src_ref=source, dst_ref=target, send_sem=ssem.at[at], recv_sem=rsem.at[at],
            device_id=peer, device_id_type=pl.DeviceIdType.MESH,
        )
        copy.start()
        started.append(copy)
        return copy

    def along_z(phase, source, target, other):
        copy = pltpu.make_async_remote_copy(
            src_ref=source, dst_ref=target,
            send_sem=zsend.at[phase, other], recv_sem=zrecv.at[phase, z],
            device_id={"rcv": other * 2 + y}, device_id_type=pl.DeviceIdType.MESH,
        )
        copy.start()

    def from_z(phase, target, other):
        pltpu.make_async_remote_copy(
            src_ref=target, dst_ref=target,
            send_sem=zsend.at[phase, other], recv_sem=zrecv.at[phase, other],
            device_id={"rcv": other * 2 + y}, device_id_type=pl.DeviceIdType.MESH,
        ).wait_recv()

    loads = [
        pltpu.make_async_copy(q_hbm.at[0, 0], a_buf.at[z, y, :, pl.ds(0, rank)], lsem.at[0]),
        pltpu.make_async_copy(q_hbm.at[1, 0], a_buf.at[z, y, :, pl.ds(rank, rank)], lsem.at[1]),
        pltpu.make_async_copy(k_hbm, k_vm, lsem.at[2]),
        pltpu.make_async_copy(d_hbm, d_vm, lsem.at[3]),
    ]
    for load in loads:
        load.start()
    barrier = pltpu.get_barrier_semaphore()
    for peer in near:
        pl.semaphore_signal(barrier, inc=1, device_id=peer, device_id_type=pl.DeviceIdType.MESH)

    def signal_z(semaphore, other):
        pl.semaphore_signal(
            semaphore, inc=1, device_id={"rcv": other * 2 + y}, device_id_type=pl.DeviceIdType.MESH
        )

    @pl.when(z > 0)
    def _():
        signal_z(barrier, z - 1)

    @pl.when(z < nz - 1)
    def _():
        signal_z(barrier, z + 1)

    beside = jnp.where(z > 0, 1, 0) + jnp.where(z < nz - 1, 1, 0)
    pl.semaphore_wait(barrier, len(near) + beside)

    def tell(k):
        @pl.when((z > 0) & (z + k < nz))
        def _():
            signal_z(upper.at[k - 1], z - 1)

        @pl.when((z < nz - 1) & (z - k >= 0))
        def _():
            signal_z(lower.at[k - 1], z + 1)

    if nz > 2:
        tell(1)
    loads[0].wait()
    loads[1].wait()

    chunk = a_buf.at[z, y]
    def halves(ref):
        return [ref.at[:, pl.ds(part * rank, rank)] for part in range(2)]

    across = [remote(chunk, chunk, ypeer)]
    for k in range(1, nz):
        @pl.when(z + k < nz)
        def _():
            if k > 1:
                pl.semaphore_wait(upper.at[k - 2], 1)
            for part, piece in enumerate(halves(chunk)):
                along_z(part, piece, piece, z + k)

        @pl.when(z - k >= 0)
        def _():
            if k > 1:
                pl.semaphore_wait(lower.at[k - 2], 1)
            for part, piece in enumerate(halves(chunk)):
                along_z(part, piece, piece, z - k)

        if 1 < k < nz - 1:
            tell(k)
    for other in far[::-1]:
        for part, piece in enumerate(halves(a_buf.at[other, y])):
            from_z(part, piece, other)
            across.append(remote(piece, piece, ypeer))

    g_loc[...] = gram(regroup(a_buf[:, y], (nz * own, 2 * rank))).reshape(2, ghalf, 2 * rank)
    g_core = remote(g_loc.at[1 - c], g_rx, cpeer)
    g_core.wait_recv()
    g_pair = g_loc[c] + g_rx[...]
    g_xtx[...] = g_pair
    g_across = [remote(g_xtx, g_xrx.at[i], peer) for i, peer in enumerate(xpeers)]

    for copy in across:
        copy.wait_recv()
    a = regroup(a_buf[...], (cols, 2 * rank))
    b = jnp.concatenate([-a[:, rank:], a[:, :rank]], axis=1)
    loads[2].wait()
    loads[3].wait()

    def product(ref, h, sign):
        at = pl.ds(pl.multiple_of(h * half, half), half)
        return dot(ref[0, at, :], a) + sign * dot(ref[1, at, :], b)

    c_tx[0] = product(k_vm, 1 - c, 1.0)
    z_core = remote(c_tx.at[0], c_rx.at[0], cpeer)
    z_own = product(k_vm, c, 1.0)
    z_core.wait_recv()
    z_own = z_own + c_rx[0]
    z_xtx[...] = z_own
    z_across = [remote(z_xtx, z_xrx.at[i], peer) for i, peer in enumerate(xpeers)]
    c_tx[1] = product(d_vm, 1 - c, -1.0)
    v_core = remote(c_tx.at[1], c_rx.at[1], cpeer)
    v_own = product(d_vm, c, -1.0)
    v_core.wait_recv()
    v_own = v_own + c_rx[1]
    v_xtx[...] = v_own.astype(BF16)
    v_across = [remote(v_xtx, v_xrx.at[i], peer) for i, peer in enumerate(xpeers)]
    for part in range(2):
        xt[:, :, :, part * rows:(part + 1) * rows] = regroup(k_vm[part].T, (nz, 2, own, rows))
        xt[:, :, :, (part + 2) * rows:(part + 3) * rows] = regroup(d_vm[part].T, (nz, 2, own, rows))
    for i, copy in enumerate(g_across):
        copy.wait_recv()
        g_pair = g_pair + g_xrx[i]
    g_ytx[...] = g_pair
    g_side = remote(g_ytx, g_yrx, ypeer)
    g_side.wait_recv()
    g_fin[c] = g_pair + g_yrx[...]
    g_back = remote(g_fin.at[c], g_fin.at[c], cpeer)
    g_back.wait_recv()
    g_high, g_low = complex_right(g_fin[...].reshape(rank, 2 * rank))
    for i, copy in enumerate(z_across):
        copy.wait_recv()
        z_own = z_own + z_xrx[i]
    z_round = z_own.astype(BF16)
    z_all[c] = z_round
    z_back = remote(z_all.at[c], z_all.at[c], cpeer)
    w_own = dot(z_round, g_high) + dot(z_round, g_low)
    z_back.wait_recv()

    z_cat = z_all[...].reshape(rows, 2 * rank)
    zr, zi = z_cat[:, :rank], z_cat[:, rank:]
    h_high, h_low = complex_right(gram(z_cat))
    z_right = jnp.concatenate(
        [jnp.concatenate([-zr, zi], axis=1), jnp.concatenate([-zi, -zr], axis=1)], axis=0
    )
    for side in range(2):
        left = regroup(xt[:, side, :, 2 * rows:], (nz * own, 2 * rows))
        q_side = regroup(a_buf[:, side], (nz * own, 2 * rank))
        total[side] = dot(left, z_right) + dot(q_side, h_high) + dot(q_side, h_low)

    for i, copy in enumerate(v_across):
        copy.wait_recv()
        v_own = v_own + v_xrx[i].astype(F32)
    w_all[c] = jnp.concatenate(
        [w_own[:, :rank] - v_own[:, :rank], w_own[:, rank:] + v_own[:, rank:]], axis=1
    ).astype(BF16)
    w_back = remote(w_all.at[c], w_all.at[c], cpeer)
    w_back.wait_recv()
    w_cat = w_all[...].reshape(rows, 2 * rank)
    wr, wi = w_cat[:, :rank], w_cat[:, rank:]
    w_right = jnp.concatenate([w_cat, jnp.concatenate([wi, -wr], axis=1)], axis=0)

    def gradient(side):
        left = regroup(xt[:, side, :, :2 * rows], (nz * own, 2 * rows))
        return (total[side] + dot(left, w_right)).reshape(nz, own, 2 * rank)

    y_tx[...] = gradient(1 - y).astype(BF16)
    to_y = [remote(y_tx.at[at], y_rx.at[at], ypeer) for at in far + [z]]
    t_tx[...] = gradient(y)
    for at, copy in zip(far, to_y):
        copy.wait_recv()
        t_rx[1, at] = (t_tx[at] + y_rx[at].astype(F32)).astype(BF16)
        along_z(2, t_rx.at[1, at], t_rx.at[0, z], at)
    to_y[-1].wait_recv()
    mine = t_tx[z] + y_rx[z].astype(F32)
    for other in far[::-1]:
        from_z(2, t_rx.at[0, other], other)
        mine = mine + t_rx[0, other].astype(F32)
    mine = mine * scaling
    o_ref[0, 0] = mine[:, :rank]
    o_ref[1, 0] = mine[:, rank:]
    for copy in started:
        copy.wait_send()
    for other in far:
        for phase, sent in enumerate(halves(a_buf.at[z, y]) + [t_rx.at[1, other]]):
            pltpu.make_async_remote_copy(
                src_ref=sent, dst_ref=sent,
                send_sem=zsend.at[phase, other], recv_sem=zrecv.at[phase, other],
                device_id={"rcv": other * 2 + y}, device_id_type=pl.DeviceIdType.MESH,
            ).wait_send()


def body(nr, ns, k_op, data, factor):
    rows, cols = k_op.shape[1:]
    own, rank = factor.shape[2:]
    nz, nx = nr // 2, ns // 2
    half = rows // 2
    count = 3 * nz + 3 * (nx - 1) + 6
    slots = max(nx - 1, 1)
    scratch = [
        pltpu.VMEM((nz, 2, own, 2 * rank), BF16),
        pltpu.VMEM((2, rows, cols), BF16),
        pltpu.VMEM((2, rows, cols), BF16),
        pltpu.VMEM((nz, 2, own, 4 * rows), BF16),
        pltpu.VMEM((2, rank // 2, 2 * rank), F32),
        pltpu.VMEM((rank // 2, 2 * rank), F32),
        pltpu.VMEM((rank // 2, 2 * rank), F32),
        pltpu.VMEM((slots, rank // 2, 2 * rank), F32),
        pltpu.VMEM((rank // 2, 2 * rank), F32),
        pltpu.VMEM((rank // 2, 2 * rank), F32),
        pltpu.VMEM((2, rank // 2, 2 * rank), F32),
        pltpu.VMEM((2, half, 2 * rank), F32),
        pltpu.VMEM((2, half, 2 * rank), F32),
        pltpu.VMEM((half, 2 * rank), F32),
        pltpu.VMEM((slots, half, 2 * rank), F32),
        pltpu.VMEM((half, 2 * rank), BF16),
        pltpu.VMEM((slots, half, 2 * rank), BF16),
        pltpu.VMEM((2, half, 2 * rank), BF16),
        pltpu.VMEM((2, half, 2 * rank), BF16),
        pltpu.VMEM((nz, own, 2 * rank), BF16),
        pltpu.VMEM((nz, own, 2 * rank), BF16),
        pltpu.VMEM((2, nz * own, 2 * rank), F32),
        pltpu.VMEM((nz, own, 2 * rank), F32),
        pltpu.VMEM((2, nz, own, 2 * rank), BF16),
        pltpu.SemaphoreType.DMA((4,)),
        pltpu.SemaphoreType.DMA((count,)),
        pltpu.SemaphoreType.DMA((count,)),
        pltpu.SemaphoreType.DMA((3, nz)),
        pltpu.SemaphoreType.DMA((3, nz)),
        pltpu.SemaphoreType.REGULAR((nz,)),
        pltpu.SemaphoreType.REGULAR((nz,)),
    ]
    scaling = 1.0 / math.sqrt(rows * nr)
    return pl.pallas_call(
        functools.partial(kernel, nz, nx, scaling),
        out_shape=jax.ShapeDtypeStruct((2, 1, own, rank), F32),
        in_specs=[pl.BlockSpec(memory_space=pl.ANY)] * 3,
        out_specs=pl.BlockSpec(memory_space=pltpu.VMEM),
        scratch_shapes=scratch,
        compiler_params=pltpu.CompilerParams(
            collective_id=0, has_side_effects=True, vmem_limit_bytes=56 * 1024 * 1024
        ),
        name="gradient",
    )(k_op, data, factor)


def solution(mesh):
    return jax.shard_map(
        functools.partial(body, mesh.shape["rcv"], mesh.shape["src"]),
        mesh=mesh,
        in_specs=(P(None, "rcv", "src"), P(None, "rcv", "src"), P(None, "src", "rcv", None)),
        out_specs=P(None, "src", "rcv", None),
        check_vma=False,
    )
```
